32 devices in a mesh: groups: 2 (over x), region: 16 (over z, y, core).
Axes of the slice: x: 2, y: 2, z: 4, core: 2. Of those that a mesh axis runs over, the one named last changes fastest.
Arguments:
- record: bfloat16 [16384, 640], P(('groups', 'region')), parts along dimension 0, may hold values from -6 to 6
- target: bfloat16 [4, 16384, 8192], P(None, ('groups', 'region')), parts along dimension 1, may hold values from -0.59765625 to 0.59765625
- offset: int32 [2], P('groups'), parts along dimension 0, may hold values from 0 to 127
- lag_steps: int32 [6], P('groups'), parts along dimension 0, may hold values from 1 to 8
Outputs:
- grad: float32 [16384, 640], P(('groups', 'region')), parts along dimension 0
The draws below stay inside these ranges and needn't reach their ends.
There are 2 independent parts, one for each index of `groups`. The reference program is written for one: setup_inputs(seed, part) draws one part's arguments, and reference() takes and returns one part's arrays. A program takes and returns all parts, laid end to end along the dimension named above; each array names one. Nothing has to cross between parts.
All inputs are finite; a program needn't handle non-finite values.
Results may differ from the reference program's by a relative error of at most 0.0005.
Values may be sent and summed in bfloat16 or wider, within the bound.
A program may use at most 256 MiB of HBM per device.

```python
import jax
import jax.numpy as jnp
from jax import lax

REGIONS = 8192
SAMPLES = 384
SLACK = 128
LAGS = 3
MAXLAG = 8
RECORD = 640


def level_of(rng, shape, pieces, smallest, largest):
    loudness = 1.0
    for axis_at, blocks in pieces:
        draws = jax.random.uniform(jax.random.fold_in(jax.random.fold_in(rng, 6), axis_at), (blocks,), jnp.float32, smallest / len(pieces), largest / len(pieces))
        loudness = loudness * jnp.repeat(jnp.exp(draws), shape[axis_at] // blocks).reshape((-1,) + (1,) * (len(shape) - 1 - axis_at))
    return loudness


def centred(own_key, shape, deviation, reach, pieces=(), dtype=jnp.bfloat16):
    array = deviation * jax.random.normal(own_key, shape, jnp.float32)
    if pieces:
        array = array * level_of(own_key, shape, pieces, -0.22, 0.18)
    return jnp.clip(array, -reach, reach).astype(dtype)


def setup_inputs(seed: int = 0, part: int = 0) -> dict:
    streams_of = jax.random.split(jax.random.key(seed), 5)
    part_keys = jax.random.split(jax.random.fold_in(streams_of[4], part), 5)
    return {
        "record": centred(part_keys[0], (REGIONS, RECORD), 1.0, 6.0, ((0, 16),)),
        "target": centred(part_keys[1], (1 + LAGS, REGIONS, REGIONS), 0.1, 0.59765625, ((1, 16),)),
        "offset": jax.random.randint(part_keys[2], (1,), 0, SLACK).astype(jnp.int32),
        "lag_steps": jax.random.randint(part_keys[3], (LAGS,), 1, MAXLAG + 1).astype(jnp.int32),
    }


def reference(record, target, offset, lag_steps):
    begin_at = offset[0].astype(jnp.int32)
    zero_index = jnp.zeros((), jnp.int32)
    early_view = lax.dynamic_slice_in_dim(record, begin_at, SAMPLES, 1)
    inverse = 1.0 / SAMPLES
    weight = SAMPLES / REGIONS
    cov_zero = jnp.dot(early_view, early_view.T, preferred_element_type=jnp.float32) * inverse
    target_zero = target[0].astype(jnp.float32)
    sym_err = (weight * (2.0 * cov_zero - target_zero - target_zero.T)).astype(jnp.bfloat16)
    grad_early = jnp.dot(sym_err, early_view, preferred_element_type=jnp.float32)
    blank = jnp.zeros((REGIONS, RECORD), jnp.float32)
    grad = jnp.zeros((REGIONS, RECORD), jnp.float32)
    for lag_number in range(LAGS):
        lag_value = lag_steps[lag_number].astype(jnp.int32)
        later_view = lax.dynamic_slice_in_dim(record, begin_at + lag_value, SAMPLES, 1)
        cov_lag = jnp.dot(early_view, later_view.T, preferred_element_type=jnp.float32) * inverse
        lag_err = (weight * (cov_lag - target[1 + lag_number].astype(jnp.float32))).astype(jnp.bfloat16)
        grad_early = grad_early + jnp.dot(lag_err, later_view, preferred_element_type=jnp.float32)
        grad_later = jnp.dot(lag_err.T, early_view, preferred_element_type=jnp.float32)
        grad = grad + lax.dynamic_update_slice(blank, grad_later, (zero_index, begin_at + lag_value))
    grad = grad + lax.dynamic_update_slice(blank, grad_early, (zero_index, begin_at))
    return grad
```

```python
import jax
import jax.numpy as jnp
from jax import lax
from jax.experimental import pallas as pl
from jax.experimental.pallas import tpu as pltpu
from jax.sharding import PartitionSpec as P

SAMPLES = 384
MAXLAG = 8
LAGS = 3
TERMS = 1 + LAGS
WIDE = 400
SPAN = SAMPLES + MAXLAG
WIDTH = 512


def placed_early(early, lag_steps):
    rows = early.shape[0]
    shifts = jnp.concatenate([jnp.zeros((1,), jnp.int32), lag_steps])
    padded = jnp.pad(early, ((0, 0), (MAXLAG, WIDE - SAMPLES)))
    parts = [
        lax.dynamic_slice(padded, (0, MAXLAG - shifts[term]), (rows, WIDE)) for term in range(TERMS)
    ]
    return jnp.stack(parts), shifts


def block_kernel(weight, scaled_ref, flat_ref, window_ref, target_ref, partial_ref, own_ref):
    rows = target_ref.shape[1]

    @pl.when(pl.program_id(0) == 0)
    def _():
        own_ref[...] = jnp.zeros_like(own_ref)

    window = window_ref[0]
    total = None
    for term in range(TERMS):
        cov = jnp.dot(scaled_ref[term], window, preferred_element_type=jnp.float32)
        error = (cov - weight * target_ref[term].astype(jnp.float32)).astype(jnp.bfloat16)
        own_ref[term] += lax.dot_general(
            window, error, (((1,), (1,)), ((), ())), preferred_element_type=jnp.float32
        )
        part = jnp.dot(
            flat_ref[:, term * rows : (term + 1) * rows], error, preferred_element_type=jnp.float32
        )
        total = part if total is None else total + part
    partial_ref[0] = total


def shards(record, target, offset, lag_steps):
    rows = record.shape[0]
    regions = target.shape[2]
    devices = lax.axis_size("region")
    begin_at = offset[0]
    window = lax.dynamic_slice_in_dim(record, begin_at, WIDE, 1)
    stacked, shifts = placed_early(window[:, :SAMPLES], lag_steps)
    scaled = stacked * jnp.bfloat16(1.0 / regions)
    flat = stacked[:, :, :SPAN].transpose(2, 0, 1).reshape(SPAN, TERMS * rows)
    turned = window.T
    gathered = lax.all_gather(turned, "region")
    blocks = regions // WIDTH
    if rows != WIDTH:
        gathered = (
            gathered.reshape(blocks, WIDTH // rows, WIDE, rows)
            .transpose(0, 2, 1, 3)
            .reshape(blocks, WIDE, WIDTH)
        )
    partials, own = pl.pallas_call(
        lambda *refs: block_kernel(SAMPLES / regions, *refs),
        grid=(blocks,),
        in_specs=[
            pl.BlockSpec((TERMS, rows, WIDE), lambda i: (0, 0, 0)),
            pl.BlockSpec((SPAN, TERMS * rows), lambda i: (0, 0)),
            pl.BlockSpec((1, WIDE, WIDTH), lambda i: (i, 0, 0)),
            pl.BlockSpec((TERMS, rows, WIDTH), lambda i: (0, 0, i)),
        ],
        out_specs=[
            pl.BlockSpec((1, SPAN, WIDTH), lambda i: (i, 0, 0)),
            pl.BlockSpec((TERMS, WIDE, rows), lambda i: (0, 0, 0)),
        ],
        out_shape=[
            jax.ShapeDtypeStruct((blocks, SPAN, WIDTH), jnp.float32),
            jax.ShapeDtypeStruct((TERMS, WIDE, rows), jnp.float32),
        ],
        compiler_params=pltpu.CompilerParams(vmem_limit_bytes=56 << 20),
        name="blocks",
    )(scaled, flat, gathered, target)
    if rows != WIDTH:
        partials = (
            partials.reshape(blocks, SPAN, WIDTH // rows, rows)
            .transpose(0, 2, 1, 3)
            .reshape(devices, SPAN, rows)
        )
    summed = lax.psum_scatter(partials, "region", scatter_dimension=0, tiled=True)[0]
    early = None
    for term in range(TERMS):
        part = lax.dynamic_slice(own[term], (shifts[term], 0), (SAMPLES, rows))
        early = part if early is None else early + part
    in_window = summed + jnp.pad(early, ((0, MAXLAG), (0, 0)))
    grad = jnp.zeros((record.shape[1], rows), jnp.float32)
    return lax.dynamic_update_slice(grad, in_window, (begin_at, 0)).T


def solution(mesh):
    placed = (
        P(("groups", "region"), None),
        P(None, ("groups", "region"), None),
        P("groups"),
        P("groups"),
    )
    return jax.shard_map(
        shards, mesh=mesh, in_specs=placed, out_specs=P(("groups", "region"), None), check_vma=False
    )
```

```python
import jax
import jax.numpy as jnp
from jax import lax
from jax.experimental import pallas as pl
from jax.experimental.pallas import tpu as pltpu
from jax.sharding import PartitionSpec as P

SAMPLES = 384
MAXLAG = 8
LAGS = 3
TERMS = 1 + LAGS
WIDE = 400
SPAN = SAMPLES + MAXLAG
WIDTH = 512


def placed_early(early, lag_steps):
    rows = early.shape[0]
    shifts = jnp.concatenate([jnp.zeros((1,), jnp.int32), lag_steps])
    padded = jnp.pad(early, ((0, 0), (MAXLAG, WIDE - SAMPLES)))
    parts = [
        lax.dynamic_slice(padded, (0, MAXLAG - shifts[term]), (rows, WIDE)) for term in range(TERMS)
    ]
    return jnp.stack(parts), shifts


def block_kernel(weight, scaled_ref, flat_ref, window_ref, target_ref, partial_ref, own_ref):
    rows = target_ref.shape[1]

    @pl.when(pl.program_id(0) == 0)
    def _():
        own_ref[...] = jnp.zeros_like(own_ref)

    window = window_ref[0]
    total = None
    for term in range(TERMS):
        cov = jnp.dot(scaled_ref[term], window, preferred_element_type=jnp.float32)
        error = (cov - weight * target_ref[term].astype(jnp.float32)).astype(jnp.bfloat16)
        own_ref[term] += lax.dot_general(
            window, error, (((1,), (1,)), ((), ())), preferred_element_type=jnp.float32
        )
        part = jnp.dot(
            flat_ref[:, term * rows : (term + 1) * rows], error, preferred_element_type=jnp.float32
        )
        total = part if total is None else total + part
    partial_ref[0] = total


def ring_place(index, count):
    chips = count // 4
    core = lax.rem(index, 2)
    low = lax.rem(lax.div(index, 2), 2)
    high = lax.div(index, 4)
    return 2 * (high + low * (2 * chips - 1 - 2 * high)) + core


def ring_index(place, count):
    chips = count // 4
    chip = lax.div(place, 2)
    low = lax.div(chip, chips)
    high = chip + low * (2 * chips - 1 - 2 * chip)
    return 4 * high + 2 * low + lax.rem(place, 2)


def ring_kernel(
    count,
    weight,
    scaled_ref,
    flat_ref,
    turned_ref,
    target_ref,
    summed_ref,
    own_ref,
    windows,
    sums,
    tiles,
    local_ref,
    tile_sem,
    window_send,
    window_recv,
    sum_send,
    sum_recv,
):
    rows = target_ref.shape[1]
    half = rows // 2
    group = lax.axis_index("groups")
    place = ring_place(lax.axis_index("region"), count)
    after = ring_index(lax.rem(place + 1, count), count)
    before = ring_index(lax.rem(place + count - 1, count), count)
    nexts = ((group, after), (group, before))

    def window_copy(step, side):
        return pltpu.make_async_remote_copy(
            src_ref=windows.at[step, side],
            dst_ref=windows.at[step + 1, side],
            send_sem=window_send.at[step, side],
            recv_sem=window_recv.at[step + 1, side],
            device_id=nexts[side],
            device_id_type=pl.DeviceIdType.MESH,
        )

    def sum_copy(step, side):
        return pltpu.make_async_remote_copy(
            src_ref=sums.at[step, side],
            dst_ref=sums.at[step + 1, side],
            send_sem=sum_send.at[step, side],
            recv_sem=sum_recv.at[step + 1, side],
            device_id=nexts[side],
            device_id_type=pl.DeviceIdType.MESH,
        )

    def tile_copy(step, side):
        moved = (count - step, step)[side]
        block = ring_index(lax.rem(place + moved, count), count)
        column = pl.multiple_of(block * rows + side * half, half)
        slot = lax.rem(step, 2)
        return pltpu.make_async_copy(
            target_ref.at[:, :, pl.ds(column, half)],
            tiles.at[slot, side],
            tile_sem.at[slot, side],
        )

    for side in range(2):
        tile_copy(0, side).start()
    windows[0] = turned_ref[...]
    own_ref[...] = jnp.zeros_like(own_ref)

    barrier = pltpu.get_barrier_semaphore()
    for side in range(2):
        pl.semaphore_signal(
            barrier, inc=1, device_id=nexts[side], device_id_type=pl.DeviceIdType.MESH
        )
    pl.semaphore_wait(barrier, 2)
    for side in range(2):
        window_copy(0, side).start()

    def visit(step, carry):
        @pl.when(step < count - 1)
        def _():
            for side in range(2):
                tile_copy(step + 1, side).start()

        for side in range(2):
            tile_copy(step, side).wait()
        slot = lax.rem(step, 2)
        window = jnp.concatenate([windows[step, 0], windows[step, 1]], axis=1)
        total = None
        for term in range(TERMS):
            tile = jnp.concatenate([tiles[slot, 0, term], tiles[slot, 1, term]], axis=1)
            cov = jnp.dot(scaled_ref[term], window, preferred_element_type=jnp.float32)
            error = (cov - weight * tile.astype(jnp.float32)).astype(jnp.bfloat16)
            own_ref[term] += lax.dot_general(
                window, error, (((1,), (1,)), ((), ())), preferred_element_type=jnp.float32
            )
            part = jnp.dot(
                flat_ref[:, term * rows : (term + 1) * rows],
                error,
                preferred_element_type=jnp.float32,
            )
            total = part if total is None else total + part
        for side in range(2):
            local_ref[side] = total[:, side * half : (side + 1) * half]

        @pl.when(step < count - 1)
        def _():
            for side in range(2):
                window_copy(step, side).wait_recv()

        @pl.when(step < count - 2)
        def _():
            for side in range(2):
                window_copy(step + 1, side).start()

        @pl.when(step <= 1)
        def _():
            sums[step] = local_ref[...]

        @pl.when(step > 1)
        def _():
            for side in range(2):
                sum_copy(step - 1, side).wait_recv()
                sums[step, side] += local_ref[side]

        @pl.when(step > 0)
        def _():
            for side in range(2):
                sum_copy(step, side).start()

        return carry

    lax.fori_loop(0, count, visit, 0)
    for side in range(2):
        sum_copy(count - 1, side).wait_recv()
        summed_ref[:, side * half : (side + 1) * half] = sums[count, side] + sums[0, side]

    def drain(step, carry):
        for side in range(2):
            window_copy(step, side).wait_send()
            sum_copy(step + 1, side).wait_send()
        return carry

    lax.fori_loop(0, count - 1, drain, 0)


def ring_call(count, regions, scaled, flat, turned, target):
    rows = target.shape[1]
    half = rows // 2
    work = 6 * TERMS * rows * regions * SPAN
    dma = pltpu.SemaphoreType.DMA
    return pl.pallas_call(
        lambda *refs: ring_kernel(count, SAMPLES / regions, *refs),
        in_specs=[pl.BlockSpec(memory_space=pltpu.VMEM)] * 3
        + [pl.BlockSpec(memory_space=pl.ANY)],
        out_specs=[pl.BlockSpec(memory_space=pltpu.VMEM)] * 2,
        out_shape=[
            jax.ShapeDtypeStruct((SPAN, rows), jnp.float32),
            jax.ShapeDtypeStruct((TERMS, WIDE, rows), jnp.float32),
        ],
        scratch_shapes=[
            pltpu.VMEM((count, 2, WIDE, half), jnp.bfloat16),
            pltpu.VMEM((count + 1, 2, SPAN, half), jnp.float32),
            pltpu.VMEM((2, 2, TERMS, rows, half), jnp.bfloat16),
            pltpu.VMEM((2, SPAN, half), jnp.float32),
            dma((2, 2)),
            dma((count, 2)),
            dma((count, 2)),
            dma((count + 1, 2)),
            dma((count + 1, 2)),
        ],
        compiler_params=pltpu.CompilerParams(
            collective_id=0, has_side_effects=True, vmem_limit_bytes=58 << 20
        ),
        cost_estimate=pl.CostEstimate(flops=work, bytes_accessed=40 << 20, transcendentals=0),
        name="ring",
    )(scaled, flat, turned, target)


def gather_call(regions, devices, scaled, flat, turned, target):
    rows = target.shape[1]
    gathered = lax.all_gather(turned, "region")
    blocks = regions // WIDTH
    if rows != WIDTH:
        gathered = (
            gathered.reshape(blocks, WIDTH // rows, WIDE, rows)
            .transpose(0, 2, 1, 3)
            .reshape(blocks, WIDE, WIDTH)
        )
    partials, own = pl.pallas_call(
        lambda *refs: block_kernel(SAMPLES / regions, *refs),
        grid=(blocks,),
        in_specs=[
            pl.BlockSpec((TERMS, rows, WIDE), lambda i: (0, 0, 0)),
            pl.BlockSpec((SPAN, TERMS * rows), lambda i: (0, 0)),
            pl.BlockSpec((1, WIDE, WIDTH), lambda i: (i, 0, 0)),
            pl.BlockSpec((TERMS, rows, WIDTH), lambda i: (0, 0, i)),
        ],
        out_specs=[
            pl.BlockSpec((1, SPAN, WIDTH), lambda i: (i, 0, 0)),
            pl.BlockSpec((TERMS, WIDE, rows), lambda i: (0, 0, 0)),
        ],
        out_shape=[
            jax.ShapeDtypeStruct((blocks, SPAN, WIDTH), jnp.float32),
            jax.ShapeDtypeStruct((TERMS, WIDE, rows), jnp.float32),
        ],
        compiler_params=pltpu.CompilerParams(vmem_limit_bytes=56 << 20),
        name="blocks",
    )(scaled, flat, gathered, target)
    if rows != WIDTH:
        partials = (
            partials.reshape(blocks, SPAN, WIDTH // rows, rows)
            .transpose(0, 2, 1, 3)
            .reshape(devices, SPAN, rows)
        )
    summed = lax.psum_scatter(partials, "region", scatter_dimension=0, tiled=True)[0]
    return summed, own


def shards(record, target, offset, lag_steps):
    rows = record.shape[0]
    regions = target.shape[2]
    devices = lax.axis_size("region")
    begin_at = offset[0]
    window = lax.dynamic_slice_in_dim(record, begin_at, WIDE, 1)
    stacked, shifts = placed_early(window[:, :SAMPLES], lag_steps)
    scaled = stacked * jnp.bfloat16(1.0 / regions)
    flat = stacked[:, :, :SPAN].transpose(2, 0, 1).reshape(SPAN, TERMS * rows)
    turned = window.T
    if rows == WIDTH:
        halves = turned.reshape(WIDE, 2, rows // 2).transpose(1, 0, 2)
        summed, own = ring_call(devices, regions, scaled, flat, halves, target)
    else:
        summed, own = gather_call(regions, devices, scaled, flat, turned, target)
    early = None
    for term in range(TERMS):
        part = lax.dynamic_slice(own[term], (shifts[term], 0), (SAMPLES, rows))
        early = part if early is None else early + part
    in_window = summed + jnp.pad(early, ((0, MAXLAG), (0, 0)))
    grad = jnp.zeros((record.shape[1], rows), jnp.float32)
    return lax.dynamic_update_slice(grad, in_window, (begin_at, 0)).T


def solution(mesh):
    placed = (
        P(("groups", "region"), None),
        P(None, ("groups", "region"), None),
        P("groups"),
        P("groups"),
    )
    return jax.shard_map(
        shards, mesh=mesh, in_specs=placed, out_specs=P(("groups", "region"), None), check_vma=False
    )
```

```python
import jax
import jax.numpy as jnp
from jax import lax
from jax.experimental import pallas as pl
from jax.experimental.pallas import tpu as pltpu
from jax.sharding import PartitionSpec as P

SAMPLES = 384
MAXLAG = 8
LAGS = 3
TERMS = 1 + LAGS
WIDE = 400
SPAN = SAMPLES + MAXLAG
WIDTH = 512
CHUNKS = ((0, 104), (104, 96), (200, 96), (296, 96))


def placed_early(early, lag_steps):
    rows = early.shape[0]
    shifts = jnp.concatenate([jnp.zeros((1,), jnp.int32), lag_steps])
    padded = jnp.pad(early, ((0, 0), (MAXLAG, WIDE - SAMPLES)))
    parts = [
        lax.dynamic_slice(padded, (0, MAXLAG - shifts[term]), (rows, WIDE)) for term in range(TERMS)
    ]
    return jnp.stack(parts), shifts


def block_kernel(weight, scaled_ref, flat_ref, window_ref, target_ref, partial_ref, own_ref):
    rows = target_ref.shape[1]

    @pl.when(pl.program_id(0) == 0)
    def _():
        own_ref[...] = jnp.zeros_like(own_ref)

    window = window_ref[0]
    total = None
    for term in range(TERMS):
        cov = jnp.dot(scaled_ref[term], window, preferred_element_type=jnp.float32)
        error = (cov - weight * target_ref[term].astype(jnp.float32)).astype(jnp.bfloat16)
        own_ref[term] += lax.dot_general(
            window, error, (((1,), (1,)), ((), ())), preferred_element_type=jnp.float32
        )
        part = jnp.dot(
            flat_ref[:, term * rows : (term + 1) * rows], error, preferred_element_type=jnp.float32
        )
        total = part if total is None else total + part
    partial_ref[0] = total


def ring_place(index, count):
    chips = count // 4
    core = lax.rem(index, 2)
    low = lax.rem(lax.div(index, 2), 2)
    high = lax.div(index, 4)
    return 2 * (high + low * (2 * chips - 1 - 2 * high)) + core


def ring_index(place, count):
    chips = count // 4
    chip = lax.div(place, 2)
    low = lax.div(chip, chips)
    high = chip + low * (2 * chips - 1 - 2 * chip)
    return 4 * high + 2 * low + lax.rem(place, 2)


def ring_kernel(
    count,
    weight,
    scaled_ref,
    flat_ref,
    turned_ref,
    target_ref,
    summed_ref,
    own_ref,
    windows,
    sums,
    tiles,
    local_ref,
    tile_sem,
    window_send,
    window_recv,
    sum_send,
    sum_recv,
):
    rows = target_ref.shape[1]
    half = rows // 2
    group = lax.axis_index("groups")
    place = ring_place(lax.axis_index("region"), count)
    after = ring_index(lax.rem(place + 1, count), count)
    before = ring_index(lax.rem(place + count - 1, count), count)
    nexts = ((group, after), (group, before))

    def window_copy(step, side):
        return pltpu.make_async_remote_copy(
            src_ref=windows.at[step, side],
            dst_ref=windows.at[step + 1, side],
            send_sem=window_send.at[step, side],
            recv_sem=window_recv.at[step + 1, side],
            device_id=nexts[side],
            device_id_type=pl.DeviceIdType.MESH,
        )

    def sum_copy(step, side, chunk):
        lines = pl.ds(*CHUNKS[chunk])
        return pltpu.make_async_remote_copy(
            src_ref=sums.at[step, side, lines],
            dst_ref=sums.at[step + 1, side, lines],
            send_sem=sum_send.at[step, side, chunk],
            recv_sem=sum_recv.at[step + 1, side, chunk],
            device_id=nexts[side],
            device_id_type=pl.DeviceIdType.MESH,
        )

    def tile_copy(step, side):
        moved = (count - step, step)[side]
        block = ring_index(lax.rem(place + moved, count), count)
        column = pl.multiple_of(block * rows + side * half, half)
        slot = lax.rem(step, 2)
        return pltpu.make_async_copy(
            target_ref.at[:, :, pl.ds(column, half)],
            tiles.at[slot, side],
            tile_sem.at[slot, side],
        )

    for side in range(2):
        tile_copy(0, side).start()
    windows[0] = turned_ref[...]
    own_ref[...] = jnp.zeros_like(own_ref)

    barrier = pltpu.get_barrier_semaphore()
    for side in range(2):
        pl.semaphore_signal(
            barrier, inc=1, device_id=nexts[side], device_id_type=pl.DeviceIdType.MESH
        )
    pl.semaphore_wait(barrier, 2)
    for side in range(2):
        window_copy(0, side).start()

    def visit(step, carry):
        @pl.when(step < count - 1)
        def _():
            for side in range(2):
                tile_copy(step + 1, side).start()

        for side in range(2):
            tile_copy(step, side).wait()
        slot = lax.rem(step, 2)
        window = jnp.concatenate([windows[step, 0], windows[step, 1]], axis=1)
        total = None
        for term in range(TERMS):
            tile = jnp.concatenate([tiles[slot, 0, term], tiles[slot, 1, term]], axis=1)
            cov = jnp.dot(scaled_ref[term], window, preferred_element_type=jnp.float32)
            error = (cov - weight * tile.astype(jnp.float32)).astype(jnp.bfloat16)
            own_ref[term] += lax.dot_general(
                window, error, (((1,), (1,)), ((), ())), preferred_element_type=jnp.float32
            )
            part = jnp.dot(
                flat_ref[:, term * rows : (term + 1) * rows],
                error,
                preferred_element_type=jnp.float32,
            )
            total = part if total is None else total + part
        for side in range(2):
            local_ref[side] = total[:, side * half : (side + 1) * half]

        @pl.when(step <= 1)
        def _():
            sums[step] = local_ref[...]

        @pl.when(step == 1)
        def _():
            for chunk in range(len(CHUNKS)):
                for side in range(2):
                    sum_copy(step, side, chunk).start()

        @pl.when(step > 1)
        def _():
            for chunk, (first, size) in enumerate(CHUNKS):
                lines = pl.ds(first, size)
                for side in range(2):
                    sum_copy(step - 1, side, chunk).wait_recv()
                    sums[step, side, lines] += local_ref[side, lines]
                    sum_copy(step, side, chunk).start()

        @pl.when(step < count - 1)
        def _():
            for side in range(2):
                window_copy(step, side).wait_recv()

        @pl.when(step < count - 2)
        def _():
            for side in range(2):
                window_copy(step + 1, side).start()

        return carry

    lax.fori_loop(0, count, visit, 0)
    for side in range(2):
        for chunk in range(len(CHUNKS)):
            sum_copy(count - 1, side, chunk).wait_recv()
        summed_ref[:, side * half : (side + 1) * half] = sums[count, side] + sums[0, side]

    def drain(step, carry):
        for side in range(2):
            window_copy(step, side).wait_send()
            for chunk in range(len(CHUNKS)):
                sum_copy(step + 1, side, chunk).wait_send()
        return carry

    lax.fori_loop(0, count - 1, drain, 0)


def ring_call(count, regions, scaled, flat, turned, target):
    rows = target.shape[1]
    half = rows // 2
    work = 6 * TERMS * rows * regions * SPAN
    dma = pltpu.SemaphoreType.DMA
    return pl.pallas_call(
        lambda *refs: ring_kernel(count, SAMPLES / regions, *refs),
        in_specs=[pl.BlockSpec(memory_space=pltpu.VMEM)] * 3
        + [pl.BlockSpec(memory_space=pl.ANY)],
        out_specs=[pl.BlockSpec(memory_space=pltpu.VMEM)] * 2,
        out_shape=[
            jax.ShapeDtypeStruct((SPAN, rows), jnp.float32),
            jax.ShapeDtypeStruct((TERMS, WIDE, rows), jnp.float32),
        ],
        scratch_shapes=[
            pltpu.VMEM((count, 2, WIDE, half), jnp.bfloat16),
            pltpu.VMEM((count + 1, 2, SPAN, half), jnp.float32),
            pltpu.VMEM((2, 2, TERMS, rows, half), jnp.bfloat16),
            pltpu.VMEM((2, SPAN, half), jnp.float32),
            dma((2, 2)),
            dma((count, 2)),
            dma((count, 2)),
            dma((count + 1, 2, len(CHUNKS))),
            dma((count + 1, 2, len(CHUNKS))),
        ],
        compiler_params=pltpu.CompilerParams(
            collective_id=0, has_side_effects=True, vmem_limit_bytes=58 << 20
        ),
        cost_estimate=pl.CostEstimate(flops=work, bytes_accessed=40 << 20, transcendentals=0),
        name="ring",
    )(scaled, flat, turned, target)


def prepare_kernel(scale, offset_ref, lag_ref, record_ref, scaled_ref, flat_ref, turned_ref):
    rows, length = record_ref.shape
    half = rows // 2
    back = lax.rem(length - offset_ref[0], length)
    window = pltpu.roll(record_ref[...].astype(jnp.float32), back, 1)[:, :WIDTH]
    turned = window.T
    for side in range(2):
        turned_ref[side] = turned[:WIDE, side * half : (side + 1) * half].astype(jnp.bfloat16)
    inside = lax.broadcasted_iota(jnp.int32, window.shape, 1) < SAMPLES
    early = jnp.where(inside, window * scale, 0.0)
    inside = lax.broadcasted_iota(jnp.int32, turned.shape, 0) < SAMPLES
    early_turned = jnp.where(inside, turned, 0.0)
    for term in range(TERMS):
        shifted, shifted_turned = early, early_turned
        if term:
            shifted = pltpu.roll(early, lag_ref[term - 1], 1)
            shifted_turned = pltpu.roll(early_turned, lag_ref[term - 1], 0)
        scaled_ref[term] = shifted[:, :WIDE].astype(jnp.bfloat16)
        flat_ref[:, term * rows : (term + 1) * rows] = shifted_turned[:SPAN].astype(jnp.bfloat16)


def finish_kernel(offset_ref, lag_ref, summed_ref, own_ref, grad_ref):
    rows, length = grad_ref.shape
    early = own_ref[0, :SAMPLES, :]
    for term in range(1, TERMS):
        early = early + pltpu.roll(own_ref[term], WIDE - lag_ref[term - 1], 0)[:SAMPLES]
    padded = jnp.concatenate(
        [
            summed_ref[:SAMPLES] + early,
            summed_ref[SAMPLES:],
            jnp.zeros((length - SPAN, rows), jnp.float32),
        ],
        axis=0,
    )
    grad_ref[...] = pltpu.roll(padded.T, offset_ref[0], 1)


def ring_shards(record, target, offset, lag_steps):
    rows, length = record.shape
    regions = target.shape[2]
    vmem = pl.BlockSpec(memory_space=pltpu.VMEM)
    smem = pl.BlockSpec(memory_space=pltpu.SMEM)
    scaled, flat, turned = pl.pallas_call(
        lambda *refs: prepare_kernel(1.0 / regions, *refs),
        in_specs=[smem, smem, vmem],
        out_specs=[vmem] * 3,
        out_shape=[
            jax.ShapeDtypeStruct((TERMS, rows, WIDE), jnp.bfloat16),
            jax.ShapeDtypeStruct((SPAN, TERMS * rows), jnp.bfloat16),
            jax.ShapeDtypeStruct((2, WIDE, rows // 2), jnp.bfloat16),
        ],
        compiler_params=pltpu.CompilerParams(vmem_limit_bytes=60 << 20),
        name="prepare",
    )(offset, lag_steps, record)
    devices = lax.axis_size("region")
    summed, own = ring_call(devices, regions, scaled, flat, turned, target)
    return pl.pallas_call(
        finish_kernel,
        in_specs=[smem, smem, vmem, vmem],
        out_specs=vmem,
        out_shape=jax.ShapeDtypeStruct((rows, length), jnp.float32),
        compiler_params=pltpu.CompilerParams(vmem_limit_bytes=60 << 20),
        name="finish",
    )(offset, lag_steps, summed, own)


def gather_call(regions, devices, scaled, flat, turned, target):
    rows = target.shape[1]
    gathered = lax.all_gather(turned, "region")
    blocks = regions // WIDTH
    if rows != WIDTH:
        gathered = (
            gathered.reshape(blocks, WIDTH // rows, WIDE, rows)
            .transpose(0, 2, 1, 3)
            .reshape(blocks, WIDE, WIDTH)
        )
    partials, own = pl.pallas_call(
        lambda *refs: block_kernel(SAMPLES / regions, *refs),
        grid=(blocks,),
        in_specs=[
            pl.BlockSpec((TERMS, rows, WIDE), lambda i: (0, 0, 0)),
            pl.BlockSpec((SPAN, TERMS * rows), lambda i: (0, 0)),
            pl.BlockSpec((1, WIDE, WIDTH), lambda i: (i, 0, 0)),
            pl.BlockSpec((TERMS, rows, WIDTH), lambda i: (0, 0, i)),
        ],
        out_specs=[
            pl.BlockSpec((1, SPAN, WIDTH), lambda i: (i, 0, 0)),
            pl.BlockSpec((TERMS, WIDE, rows), lambda i: (0, 0, 0)),
        ],
        out_shape=[
            jax.ShapeDtypeStruct((blocks, SPAN, WIDTH), jnp.float32),
            jax.ShapeDtypeStruct((TERMS, WIDE, rows), jnp.float32),
        ],
        compiler_params=pltpu.CompilerParams(vmem_limit_bytes=56 << 20),
        name="blocks",
    )(scaled, flat, gathered, target)
    if rows != WIDTH:
        partials = (
            partials.reshape(blocks, SPAN, WIDTH // rows, rows)
            .transpose(0, 2, 1, 3)
            .reshape(devices, SPAN, rows)
        )
    summed = lax.psum_scatter(partials, "region", scatter_dimension=0, tiled=True)[0]
    return summed, own


def shards(record, target, offset, lag_steps):
    rows = record.shape[0]
    if rows == WIDTH:
        return ring_shards(record, target, offset, lag_steps)
    regions = target.shape[2]
    devices = lax.axis_size("region")
    begin_at = offset[0]
    window = lax.dynamic_slice_in_dim(record, begin_at, WIDE, 1)
    stacked, shifts = placed_early(window[:, :SAMPLES], lag_steps)
    scaled = stacked * jnp.bfloat16(1.0 / regions)
    flat = stacked[:, :, :SPAN].transpose(2, 0, 1).reshape(SPAN, TERMS * rows)
    turned = window.T
    summed, own = gather_call(regions, devices, scaled, flat, turned, target)
    early = None
    for term in range(TERMS):
        part = lax.dynamic_slice(own[term], (shifts[term], 0), (SAMPLES, rows))
        early = part if early is None else early + part
    in_window = summed + jnp.pad(early, ((0, MAXLAG), (0, 0)))
    grad = jnp.zeros((record.shape[1], rows), jnp.float32)
    return lax.dynamic_update_slice(grad, in_window, (begin_at, 0)).T


def solution(mesh):
    placed = (
        P(("groups", "region"), None),
        P(None, ("groups", "region"), None),
        P("groups"),
        P("groups"),
    )
    return jax.shard_map(
        shards, mesh=mesh, in_specs=placed, out_specs=P(("groups", "region"), None), check_vma=False
    )
```
